32 devices in a mesh: sect: 2 (over y), op: 16 (over z, x, core).
Axes of the slice: x: 2, y: 2, z: 4, core: 2. Of those that a mesh axis runs over, the one named last changes fastest.
Arguments:
- wave: bfloat16 [2, 8192, 256], P('sect', 'op'), may hold values from -6 to 6
- left_ops: bfloat16 [2, 48, 8, 256, 256], P('sect', 'op'), may hold values from -0.5 to 0.5
- right_ops: bfloat16 [2, 48, 8, 256, 256], P('sect', 'op'), may hold values from -0.375 to 0.375
- site_ops: float32 [2, 48, 4, 4], P('sect', 'op'), may hold values from -0.4375 to 0.4375
- reach: int32 [2, 48], P('sect', 'op'), may hold values from 1 to 8
- pairing: int32 [2, 8], P('sect'), may hold values from 0 to 7, each once within a row
- site_tensor: bfloat16 [2, 8, 4, 256, 256], P('sect'), may hold values from -0.25 to 0.25
Outputs:
- first_image: bfloat16 [2, 8192, 256], P('sect', 'op')
- second_image: bfloat16 [2, 8192, 256], P('sect', 'op')
- moved_image: bfloat16 [2, 8192, 256], P('sect', 'op')
The draws below stay inside these ranges and needn't reach their ends.
Inputs may be any that keep to these rules, and one draw needn't show every extreme that they name: Each term couples the sectors 0 to reach - 1. `pairing`: each row is a permutation of the 8 sectors.
All inputs are finite; a program needn't handle non-finite values.
Results may differ from the reference program's by a relative error of at most 0.008.
Values may be sent and summed in bfloat16 or wider, within the bound.
A program may use at most 128 MiB of HBM per device.

```python
import jax
import jax.numpy as jnp
from jax import lax

SECTORS = 8
BLOCK = 256
LOCAL = 4
SECTIONS = 2
TERMS = 48
ROWS = 8192


def plant(result, own_key, least, top_value):
    dims = result.shape
    index_at = [jax.random.randint(jax.random.fold_in(own_key, axis), (), 0, dims[axis]) for axis in range(len(dims))]
    result = result.at[tuple(index_at)].set(least)
    longest = dims.index(max(dims))
    index_at[longest] = (index_at[longest] + 1) % dims[longest]
    return result.at[tuple(index_at)].set(top_value)


def with_spikes(entries, key, source, target, parts, factor):
    def block_of(position):
        return (jnp.arange(entries.shape[position]) // (entries.shape[position] // parts)).reshape((-1,) + (1,) * (entries.ndim - 1 - position))

    one_side = jax.random.permutation(key, parts)[block_of(target)]
    far = (block_of(target) + parts // 2) % parts
    return jnp.where((block_of(source) == one_side) | (block_of(source) == far), factor * entries, entries)


def block_levels(key, shape, shards, smallest, top_value):
    def one(axis_at, parts):
        heights = jax.random.uniform(jax.random.fold_in(jax.random.fold_in(key, 6), axis_at), (parts,), jnp.float32, smallest / len(shards), top_value / len(shards))
        return jnp.repeat(jnp.exp(heights), shape[axis_at] // parts).reshape((-1,) + (1,) * (len(shape) - axis_at - 1))

    factor_of = one(*shards[0])
    for cut in shards[1:]:
        factor_of = factor_of * one(*cut)
    return factor_of


def scatter_about(key, extent, deviation, most, cuts=(), kind=jnp.bfloat16):
    array = deviation * jax.random.normal(key, extent, jnp.float32)
    if cuts:
        array = array * block_levels(key, extent, cuts, -0.22, 0.18)
    return jnp.clip(array, -most, most).astype(kind)


def heavy_noise(stream_key, extent, deviation, most, cuts, heavy, kind=jnp.bfloat16):
    values = deviation * jax.random.normal(stream_key, extent, jnp.float32)
    if cuts:
        values = values * block_levels(stream_key, extent, cuts, -0.22, 0.18)
    return jnp.clip(with_spikes(values, jax.random.fold_in(stream_key, 3), *heavy), -most, most).astype(kind)


def setup_inputs(seed: int = 0) -> dict:
    arg_keys = jax.random.split(jax.random.key(seed), 8)
    return {
        "wave": scatter_about(arg_keys[0], (SECTIONS, ROWS, BLOCK), 1.0, 6.0, ((0, 2), (1, 16))),
        "left_ops": heavy_noise(arg_keys[1], (SECTIONS, TERMS, SECTORS, BLOCK, BLOCK), BLOCK ** -0.5, 0.5, ((0, 2), (1, 16)), (1, 3, 16, 2.0)),
        "right_ops": scatter_about(arg_keys[2], (SECTIONS, TERMS, SECTORS, BLOCK, BLOCK), BLOCK ** -0.5, 0.375, ((0, 2), (1, 16))),
        "site_ops": scatter_about(arg_keys[3], (SECTIONS, TERMS, LOCAL, LOCAL), (LOCAL * TERMS) ** -0.5, 0.4375, ((0, 2), (1, 16)), jnp.float32),
        "reach": plant(jax.random.randint(arg_keys[4], (SECTIONS, TERMS), 1, SECTORS + 1), jax.random.fold_in(arg_keys[4], 1), 1, SECTORS).astype(jnp.int32),
        "pairing": jax.vmap(lambda own: jax.random.permutation(own, SECTORS))(jax.random.split(arg_keys[5], SECTIONS)).reshape((SECTIONS, SECTORS)).astype(jnp.int32),
        "site_tensor": scatter_about(arg_keys[6], (SECTIONS, SECTORS, LOCAL, BLOCK, BLOCK), (2 * BLOCK) ** -0.5, 0.25, ((0, 2),)),
    }


def apply_terms(wave, lefts, rights, mixers, limits, pair):
    sector_ids = jnp.arange(SECTORS, dtype=jnp.int32)
    wave_f = wave.astype(jnp.float32)

    def one_term(total, term):
        left, right, mixer, limit = term
        lifted = jnp.einsum("qab,qsbc->qsac", left.astype(jnp.float32), wave_f).astype(jnp.bfloat16)
        mask = (sector_ids < limit).astype(jnp.float32)
        mixed = jnp.einsum("xy,qyac->qxac", mixer, lifted.astype(jnp.float32), precision=lax.Precision.HIGHEST)
        mixed = (mixed * mask[:, None, None, None]).astype(jnp.bfloat16)
        paired = jnp.take(right, pair, axis=0).astype(jnp.float32)
        return total + jnp.einsum("qsac,qdc->qsad", mixed.astype(jnp.float32), paired), None

    start = jnp.zeros((SECTORS, LOCAL, BLOCK, BLOCK), jnp.float32)
    total, unused = lax.scan(one_term, start, (lefts, rights, mixers, limits))
    return total.astype(jnp.bfloat16)


def renormalize(lefts, tensor, pair):
    onehot = (pair[:, None] == jnp.arange(SECTORS, dtype=jnp.int32)[None, :]).astype(jnp.float32)
    tensor_f = tensor.astype(jnp.float32)

    def one_term(carry, left):
        lifted = jnp.einsum("qab,qsbc->qsac", left.astype(jnp.float32), tensor_f).astype(jnp.bfloat16)
        reduced = jnp.einsum("qsad,qsac->qdc", tensor_f, lifted.astype(jnp.float32)).astype(jnp.bfloat16)
        placed = jnp.einsum("qj,qdc->jdc", onehot, reduced.astype(jnp.float32), precision=lax.Precision.HIGHEST)
        return carry, placed.astype(jnp.bfloat16)

    unused, renewed = lax.scan(one_term, jnp.zeros((), jnp.float32), lefts)
    return renewed


def reference(wave, left_ops, right_ops, site_ops, reach, pairing, site_tensor):
    firsts = []
    seconds = []
    renewed = []
    for section in range(SECTIONS):
        blocks = wave[section].reshape(SECTORS, LOCAL, BLOCK, BLOCK)
        first = apply_terms(blocks, left_ops[section], right_ops[section], site_ops[section], reach[section], pairing[section])
        second = apply_terms(first, left_ops[section], right_ops[section], site_ops[section], reach[section], pairing[section])
        firsts.append(first.reshape(ROWS, BLOCK))
        seconds.append(second.reshape(ROWS, BLOCK))
        renewed.append(renormalize(left_ops[section], site_tensor[section], pairing[section]))
    moved = []
    for section in range(SECTIONS):
        blocks = wave[section].reshape(SECTORS, LOCAL, BLOCK, BLOCK)
        image = apply_terms(blocks, renewed[section - 1], right_ops[section], site_ops[section], reach[section], pairing[section])
        moved.append(image.reshape(ROWS, BLOCK))
    return jnp.stack(firsts), jnp.stack(seconds), jnp.stack(moved)
```

```python
import functools

import jax
import jax.numpy as jnp
from jax import lax
from jax.experimental import pallas as pl
from jax.experimental.pallas import tpu as pltpu
from jax.sharding import PartitionSpec as P

SUBS = 2
BIG = 67043328
BF, F32 = jnp.bfloat16, jnp.float32


def remote(src, dst, send, recv, who):
    return pltpu.make_async_remote_copy(
        src_ref=src, dst_ref=dst, send_sem=send, recv_sem=recv, device_id=who,
        device_id_type=pl.DeviceIdType.MESH,
    )


def cond(test, body):
    if isinstance(test, bool):
        if test:
            body()
    else:
        pl.when(test)(body)


def both(a, b):
    return (a and b) if isinstance(a, bool) and isinstance(b, bool) else jnp.logical_and(a, b)


def either(a, b):
    return (a or b) if isinstance(a, bool) and isinstance(b, bool) else jnp.logical_or(a, b)


def loop(low, high, body):
    if low < high:
        lax.fori_loop(low, high, lambda i, c: body(i) or c, 0)


class Ring:
    def __init__(self, count, sections):
        me = lax.axis_index("op")
        here = lax.axis_index("sect")
        self.sections = sections
        self.ahead = {"sect": lax.rem(here + 1, sections)}
        self.behind = {"sect": lax.rem(here + sections - 1, sections)}
        self.m = count // 2
        self.half = self.m // 2
        self.core = lax.rem(me, 2)
        self.chip = lax.div(me, 2)
        odd = lax.rem(self.chip, 2)
        low = lax.div(self.chip, 2)
        self.pos = (1 - odd) * low + odd * (self.m - 1 - low)
        self.sibling = {"op": self.chip * 2 + 1 - self.core}
        self.next = [
            {"op": self.chip_at(1) * 2 + self.core},
            {"op": self.chip_at(-1) * 2 + self.core},
        ]

    def chip_at(self, offset):
        pos = lax.rem(self.pos + offset + self.m, self.m)
        upper = lax.div(pos, self.half)
        return (1 - upper) * (2 * pos) + upper * (2 * (self.m - 1 - pos) + 1)

    def chip_of(self, n):
        if isinstance(n, int):
            return self.chip_at((n + 1) // 2 * (2 * (n % 2) - 1))
        return self.chip_at(lax.div(n + 1, 2) * (2 * lax.rem(n, 2) - 1))

    def barrier(self):
        sem = pltpu.get_barrier_semaphore()
        peers = [self.next[0], self.next[1], self.sibling, self.ahead]
        if self.sections > 2:
            peers.append(self.behind)
        for who in peers:
            pl.semaphore_signal(sem, inc=1, device_id=who, device_id_type=pl.DeviceIdType.MESH)
        pl.semaphore_wait(sem, len(peers))


class Gather:
    def __init__(self, ring, whole, rows, sems):
        self.ring, self.whole, self.rows = ring, whole, rows
        self.send, self.recv, self.sib_send, self.sib_recv = sems
        self.each = ring.m // whole.shape[0]

    def at(self, chunk, first, size):
        start = (lax.rem(chunk, self.each) * 2 + self.ring.core) * self.rows + first
        return self.whole.at[lax.div(chunk, self.each), pl.ds(pl.multiple_of(start, size), size)]

    def part(self, chunk, u):
        return self.at(chunk, u * (self.rows // SUBS), self.rows // SUBS)

    def own(self):
        return self.at(self.ring.chip, 0, self.rows)

    def hop(self, d, s, u, ref):
        return remote(ref, ref, self.send.at[d, s, u], self.recv.at[d, s, u], self.ring.next[d])

    def over(self, d, s, u, ref):
        return remote(
            ref, ref, self.sib_send.at[d, s, u], self.sib_recv.at[d, s, u], self.ring.sibling
        )

    def start(self, u):
        ref = self.part(self.ring.chip, u)
        for d in range(2):
            if self.ring.half > 1 or u == d:
                self.hop(d, 0, u, ref).start()
        self.over(0, 0, u, ref).start()

    def forward(self, s, u):
        half = self.ring.half
        for d in range(2):
            ref = self.part(self.ring.chip_at(-s if d == 0 else s), u)

            def pass_on(d=d, ref=ref):
                self.hop(d, s - 1, u, ref).wait_recv()
                cond(
                    both(s < half, either(s < half - 1, u == d)),
                    lambda: self.hop(d, s, u, ref).start(),
                )
                self.over(d, s, u, ref).start()

            cond(either(s < half, u == d), pass_on)

    def ready(self, n):
        m, half = self.ring.m, self.ring.half
        ref = self.part(self.ring.chip, 0)

        def far():
            for d in range(2):
                self.over(d, half, d, ref).wait_recv()

        def near():
            d, s = lax.rem(n, 2), lax.div(n + 1, 2)
            for u in range(SUBS):
                self.over(d, s, u, ref).wait_recv()

        pl.when(n == m - 1)(far)
        pl.when(n != m - 1)(near)

    def run(self, work):
        m = self.ring.m

        def body(i):
            pl.when(i < m)(lambda: self.forward(lax.div(i, 2) + 1, lax.rem(i, 2)))

            def at(n):
                self.ready(n)

            n = jnp.maximum(i - 1, 0)
            work(i, n, lambda: pl.when(i != 1)(lambda: at(n)))

        loop(0, m + 1, body)

    def drain(self):
        half = self.ring.half
        ref = self.part(self.ring.chip, 0)
        for d in range(2):
            for u in range(SUBS):
                for s in range(half + 1):
                    if s < half and (s < half - 1 or u == d):
                        self.hop(d, s, u, ref).wait_send()
                    if (d == 0) if s == 0 else (s < half or u == d):
                        self.over(d, s, u, ref).wait_send()


class Scatter:
    def __init__(self, ring, own, give, land, buf, sems):
        self.ring, self.own, self.give, self.land, self.buf = ring, own, give, land, buf
        self.send, self.recv, self.sib_send, self.sib_recv = sems
        self.rows = own.shape[1] // SUBS

    def over(self, n, chunk):
        return remote(
            self.give.at[chunk], self.land.at[chunk], self.sib_send.at[n], self.sib_recv.at[n],
            self.ring.sibling,
        )

    def offer(self, n):
        self.over(n, self.ring.chip_of(n)).start()

    def settle(self, n):
        self.over(n, self.ring.chip).wait_recv()

    def move(self, d, j, u):
        return remote(
            self.buf.at[d, j, u], self.buf.at[d, j + 1, u], self.send.at[d, j, u],
            self.recv.at[d, j, u], self.ring.next[d],
        )

    def local(self, chunk, u):
        cut = pl.ds(pl.multiple_of(u * self.rows, self.rows), self.rows)
        return self.own[chunk, cut, :] + self.land[chunk, cut, :].astype(F32)

    def first(self):
        m, half = self.ring.m, self.ring.half
        self.settle(m - 1)
        for d in range(2):
            self.buf[d, 0, d] = self.local(self.ring.chip_at(half), d).astype(BF)
            self.move(d, 0, d).start()

    def hop(self, j, u):
        dist = self.ring.half - j

        def settle():
            self.settle(2 * dist - 1)
            self.settle(2 * dist)

        cond(u == 0, settle)
        for d in range(2):
            value = self.local(self.ring.chip_at(dist if d == 0 else -dist), u)
            has = either(j > 1, u == d)

            def add(d=d, value=value):
                self.move(d, j - 1, u).wait_recv()
                self.buf[d, j, u] = (value + self.buf[d, j, u].astype(F32)).astype(BF)

            def put(d=d, value=value):
                self.buf[d, j, u] = value.astype(BF)

            cond(has, add)
            cond((not has) if isinstance(has, bool) else jnp.logical_not(has), put)
            self.move(d, j, u).start()

    def last(self, u):
        half = self.ring.half
        if u == 0:
            self.settle(0)
        value = self.local(self.ring.chip, u)
        for d in range(2):
            if half > 1 or u == d:
                self.move(d, half - 1, u).wait_recv()
                value = value + self.buf[d, half, u].astype(F32)
        return value.astype(BF)

    def drain(self):
        for d in range(2):
            for u in range(SUBS):
                for j in range(self.ring.half):
                    if j or u == d:
                        self.move(d, j, u).wait_send()
        for n in range(self.ring.m):
            self.over(n, self.ring.chip).wait_send()


class Apply:
    def __init__(self, ring, rights, mixers, limits, pair, acc):
        self.ring, self.rights, self.acc = ring, rights, acc
        self.mixers, self.limits, self.pair = mixers, limits, pair
        self.terms, self.sectors, self.block, _ = rights.shape
        self.local = mixers.shape[2]

    def lift(self, t, q, left, v):
        return [
            jnp.dot(left, v[q, pl.ds(s * self.block, self.block), :], preferred_element_type=F32)
            .astype(BF)
            for s in range(self.local)
        ]

    def mix(self, t, q, x, lifted):
        live = jnp.where(q < self.limits[0, t], 1.0, 0.0).astype(F32)
        mixed = (live * self.mixers[0, t, x, 0]) * lifted[0].astype(F32)
        for y in range(1, self.local):
            mixed = mixed + (live * self.mixers[0, t, x, y]) * lifted[y].astype(F32)
        return mixed.astype(BF)

    def right(self, t, q, mixed):
        return lax.dot_general(
            mixed, self.rights[t, self.pair[0, q]], (((1,), (1,)), ((), ())),
            preferred_element_type=F32,
        )

    def to(self, q, v, left_of, st, given):
        per = self.local // 2
        lifted = [self.lift(t, q, left_of(t), v) for t in range(self.terms)]
        for i in range(self.local):
            core = 1 - self.ring.core if i < per else self.ring.core
            x = core * per + i % per
            total = None
            for t in range(self.terms):
                term = self.right(t, q, self.mix(t, q, x, lifted[t]))
                total = term if total is None else total + term
            rows = pl.ds(i % per * self.block, self.block)
            if i < per:
                st.give[q, rows, :] = total.astype(BF)
            else:
                st.own[q, rows, :] = total
            if i == per - 1:
                given()

    def shared(self, q, v, left_of, st):
        acc = self.acc
        for t in range(self.terms):
            lifted = self.lift(t, q, left_of(t), v)
            for x in range(self.local):
                rows = pl.ds(x * self.block, self.block)
                term = self.right(t, q, self.mix(t, q, x, lifted))
                acc[rows, :] = term if t == 0 else acc[rows, :] + term
        rows = st.own.shape[1]
        each = st.own.shape[0] // self.sectors
        core = self.ring.core
        for j in range(each):
            mine = pl.multiple_of((2 * j + core) * rows, rows)
            other = pl.multiple_of((2 * j + 1 - core) * rows, rows)
            st.own[q * each + j] = acc[pl.ds(mine, rows), :]
            st.give[q * each + j] = acc[pl.ds(other, rows), :].astype(BF)


def renew(i, j, pair, lefts, tensor, out):
    terms, sectors = lefts.shape[:2]
    local = tensor.shape[1]
    source = jnp.int32(0)
    for k in range(sectors):
        source = jnp.where(pair[0, k] == j, k, source)
    stack = jnp.concatenate([tensor[source, s] for s in range(local)], axis=0)
    for t in range(terms):
        lifted = [
            jnp.dot(lefts[t, source], tensor[source, s], preferred_element_type=F32).astype(BF)
            for s in range(local)
        ]
        out[i, t] = lax.dot_general(
            stack, jnp.concatenate(lifted, axis=0), (((0,), (0,)), ((), ())),
            preferred_element_type=F32,
        ).astype(BF)


def interleaved(chips, sectors, local):
    return chips == sectors and chips > 6 and local % 2 == 0


def whole_kernel(
    count, sections, pair, limits, mixers, wave, left_in, right_in, tensor_in,
    out1, out2, out3,
    lefts, rights, tensor, whole, image, renewed, moved, acc, stage,
    loads, writes, cross_send, cross_recv, *rest
):
    ring = Ring(count, sections)
    m, half, core = ring.m, ring.half, ring.core
    terms, sectors = rights.shape[:2]
    rows = wave.shape[0]
    tight = interleaved(m, sectors, mixers.shape[2])
    s1, s2, s3 = (
        Scatter(ring, *rest[8 * i:8 * i + 4], rest[8 * i + 4:8 * i + 8]) for i in range(3)
    )
    g1 = Gather(ring, whole, rows, rest[24:28])
    g2 = Gather(ring, image, rows, rest[28:32])
    work = Apply(ring, rights, mixers, limits, pair, acc)

    keep = pltpu.make_async_copy(wave, g1.own(), loads.at[3])
    keep.start()
    ring.barrier()
    keep.wait()
    for u in range(SUBS):
        g1.start(u)
    loaded = [
        pltpu.make_async_copy(a, b, loads.at[i])
        for i, (a, b) in enumerate(((left_in, lefts), (tensor_in, tensor), (right_in, rights)))
    ]
    for copy in loaded:
        copy.start()

    def sector_of(i):
        return ring.chip_of(m - 1 - i) if tight else i

    def crossing(i):
        return remote(
            renewed.at[i], moved.at[i], cross_send.at[i], cross_recv.at[i], ring.ahead
        )

    def renew_one(i):
        renew(i, sector_of(i), pair, lefts, tensor, renewed)
        crossing(i).start()

    def apply_to(st, v, n):
        work.to(ring.chip_of(n), v, lambda t: lefts[t, ring.chip_of(n)], st, lambda: st.offer(n))

    def apply_moved(i):
        crossing(i).wait_recv()
        n = m - 1 - i
        work.to(ring.chip_of(n), whole, lambda t: moved[i, t], s3, lambda: s3.offer(n))

    def hops(st, low, high, slot):
        def body(k):
            pl.when(k > low)(
                lambda: st.hop(1 + lax.div(k - low - 1, SUBS), lax.rem(k - low - 1, SUBS))
            )
            slot(k)

        loop(low, high, body)

    def finish(st, ref, after=lambda u: None):
        size = rows // SUBS
        for u in range(SUBS):
            ref[pl.ds(u * size, size), :] = st.last(u)
            after(u)

    def write(i, src, dst):
        pltpu.make_async_copy(src, dst, writes.at[i]).start()

    for copy in loaded:
        copy.wait()
    steps = SUBS * (half - 1) + 1
    if tight:
        def first_work(i, n, ready):
            pl.when(jnp.logical_or(i == 0, jnp.logical_and(lax.rem(i, 2) == 1, i < m - 1)))(
                lambda: renew_one(lax.div(i + 1, 2))
            )
            ready()
            pl.when(i != 1)(lambda: apply_to(s1, whole, n))

        g1.run(first_work)
        s1.first()

        def first_slot(k):
            pl.when(jnp.logical_and(k > 0, k <= half))(lambda: renew_one(half - 1 + k))
            pl.when(jnp.logical_or(k == 0, jnp.logical_and(k > half, k <= half + 2)))(
                lambda: apply_moved(jnp.maximum(k - half, 0))
            )
            pl.when(k == 0)(s3.first)

        hops(s1, 0, steps, first_slot)
        for u in range(SUBS):
            s3.hop(1, u)
        finish(s1, g2.own(), g2.start)
        write(0, g2.own(), out1)

        def second_work(i, n, ready):
            pl.when(i == m - 2)(lambda: [s3.hop(2, u) for u in range(SUBS)] and None)
            ready()
            pl.when(i != 1)(lambda: apply_to(s2, image, n))
            pl.when(jnp.logical_and(lax.rem(i, 2) == 1, i < m - 1))(
                lambda: apply_moved(3 + lax.div(i, 2))
            )

        g2.run(second_work)
        s2.first()
        done = half + 2

        def second_slot(k):
            pl.when(jnp.logical_and(lax.rem(k, 2) == 0, k < 2 * (sectors - done)))(
                lambda: apply_moved(done + lax.div(k, 2))
            )
            for j in range(3, half):
                pl.when(k == max(2 * (2 * j - done) + 1, 1))(
                    lambda j=j: [s3.hop(j, u) for u in range(SUBS)] and None
                )

        hops(s2, 0, steps, second_slot)
        finish(s3, stage.at[1])
        write(2, stage.at[1], out3)
        finish(s2, stage.at[0])
        write(1, stage.at[0], out2)
    else:
        def plain(i, n, ready):
            ready()

        def spread(st, v, left_of, before=lambda q: None):
            def body(q):
                before(q)
                work.shared(q, v, functools.partial(left_of, q), st)

            loop(0, sectors, body)
            loop(0, m, st.offer)
            st.first()
            hops(st, 0, steps, lambda k: None)

        def plain_left(q, t):
            return lefts[t, q]

        loop(0, sectors, renew_one)
        g1.run(plain)
        spread(s1, whole, plain_left)
        finish(s1, g2.own(), g2.start)
        write(0, g2.own(), out1)
        g2.run(plain)
        spread(s2, image, plain_left)
        finish(s2, stage.at[0])
        write(1, stage.at[0], out2)
        spread(s3, whole, lambda q, t: moved[q, t], lambda q: crossing(q).wait_recv())
        finish(s3, stage.at[1])
        write(2, stage.at[1], out3)
    for part in (g1, g2, s1, s2, s3):
        part.drain()
    loop(0, sectors, lambda i: crossing(i).wait_send())
    for i, out in enumerate((out1, out2, out3)):
        pltpu.make_async_copy(stage.at[0], out, writes.at[i]).wait()


def hand_out(*refs):
    ins, outs, (held, loads, writes) = refs[:3], refs[3:6], refs[6:]
    copies = [pltpu.make_async_copy(a, held.at[i], loads.at[i]) for i, a in enumerate(ins)]
    for copy in copies:
        copy.start()
    back = []
    for i, copy in enumerate(copies):
        copy.wait()
        back.append(pltpu.make_async_copy(held.at[i], outs[i], writes.at[i]))
        back[-1].start()
    for copy in back:
        copy.wait()


def gather_scratch(half):
    dma = pltpu.SemaphoreType.DMA
    hop, sib = (2, half, SUBS), (2, half + 1, SUBS)
    return [dma(hop), dma(hop), dma(sib), dma(sib)]


def scatter_scratch(chips, rows, width):
    half = chips // 2
    dma = pltpu.SemaphoreType.DMA
    hop = (2, half, SUBS)
    return [
        pltpu.VMEM((chips, rows, width), F32),
        pltpu.VMEM((chips, rows, width), BF),
        pltpu.VMEM((chips, rows, width), BF),
        pltpu.VMEM((2, half + 1, SUBS, rows // SUBS, width), BF),
        dma(hop), dma(hop), dma((chips,)), dma((chips,)),
    ]


def shards(count, sections, wave, left_ops, right_ops, site_ops, reach, pairing, site_tensor):
    lefts, rights, own, tensor = left_ops[0], right_ops[0], wave[0], site_tensor[0]
    terms, sectors, block, _ = lefts.shape
    rows, width = own.shape
    chips = count // 2
    height = count * rows // sectors
    tight = interleaved(chips, sectors, site_ops.shape[2])
    dma = pltpu.SemaphoreType.DMA
    sm = pl.BlockSpec(memory_space=pltpu.SMEM)
    anyw = pl.BlockSpec(memory_space=pl.ANY)
    image = pltpu.VMEM((sectors, height, width), BF)
    across = pltpu.VMEM((sectors, terms, block, block), BF)
    mine = jax.ShapeDtypeStruct((rows, width), BF)
    outs = pl.pallas_call(
        functools.partial(whole_kernel, count, sections),
        out_shape=[mine] * 3,
        in_specs=[sm] * 3 + [anyw] * 4,
        out_specs=[anyw] * 3,
        scratch_shapes=[
            pltpu.VMEM(lefts.shape, BF), pltpu.VMEM(rights.shape, BF),
            pltpu.VMEM(tensor.shape, BF), image, image, across, across,
            pltpu.VMEM((8, width) if tight else (height, width), F32),
            pltpu.VMEM((2, rows, width), BF),
            dma((4,)), dma((3,)), dma((sectors,)), dma((sectors,)),
        ] + scatter_scratch(chips, rows, width) * 3 + gather_scratch(chips // 2) * 2,
        compiler_params=pltpu.CompilerParams(
            collective_id=0, has_side_effects=True, vmem_limit_bytes=BIG
        ),
        name="images",
    )(pairing, reach, site_ops, own, lefts, rights, tensor)
    outs = pl.pallas_call(
        hand_out,
        out_shape=[mine] * 3,
        in_specs=[anyw] * 3,
        out_specs=[anyw] * 3,
        scratch_shapes=[pltpu.VMEM((3, rows, width), BF), dma((3,)), dma((3,))],
        name="hand_out",
    )(*outs)
    return tuple(out[None] for out in outs)


def solution(mesh):
    placed = (
        P("sect", "op", None),
        P("sect", "op", None, None, None),
        P("sect", "op", None, None, None),
        P("sect", "op", None, None),
        P("sect", "op"),
        P("sect", None),
        P("sect", None, None, None, None),
    )
    return jax.shard_map(
        functools.partial(shards, mesh.shape["op"], mesh.shape["sect"]),
        mesh=mesh,
        in_specs=placed,
        out_specs=(P("sect", "op", None), P("sect", "op", None), P("sect", "op", None)),
        check_vma=False,
    )
```

```python
import functools

import jax
import jax.numpy as jnp
from jax import lax
from jax.experimental import pallas as pl
from jax.experimental.pallas import tpu as pltpu
from jax.sharding import PartitionSpec as P

SUBS = 2
BIG = 67043328
BF, F32 = jnp.bfloat16, jnp.float32


def remote(src, dst, send, recv, who):
    return pltpu.make_async_remote_copy(
        src_ref=src, dst_ref=dst, send_sem=send, recv_sem=recv, device_id=who,
        device_id_type=pl.DeviceIdType.MESH,
    )


def cond(test, body):
    if isinstance(test, bool):
        if test:
            body()
    else:
        pl.when(test)(body)


def both(a, b):
    return (a and b) if isinstance(a, bool) and isinstance(b, bool) else jnp.logical_and(a, b)


def either(a, b):
    return (a or b) if isinstance(a, bool) and isinstance(b, bool) else jnp.logical_or(a, b)


def loop(low, high, body):
    if low < high:
        lax.fori_loop(low, high, lambda i, c: body(i) or c, 0)


class Ring:
    def __init__(self, count, sections):
        me = lax.axis_index("op")
        here = lax.axis_index("sect")
        self.sections = sections
        self.ahead = {"sect": lax.rem(here + 1, sections)}
        self.behind = {"sect": lax.rem(here + sections - 1, sections)}
        self.m = count // 2
        self.half = self.m // 2
        self.core = lax.rem(me, 2)
        self.chip = lax.div(me, 2)
        odd = lax.rem(self.chip, 2)
        low = lax.div(self.chip, 2)
        self.pos = (1 - odd) * low + odd * (self.m - 1 - low)
        self.sibling = {"op": self.chip * 2 + 1 - self.core}
        self.next = [
            {"op": self.chip_at(1) * 2 + self.core},
            {"op": self.chip_at(-1) * 2 + self.core},
        ]

    def chip_at(self, offset):
        pos = lax.rem(self.pos + offset + self.m, self.m)
        upper = lax.div(pos, self.half)
        return (1 - upper) * (2 * pos) + upper * (2 * (self.m - 1 - pos) + 1)

    def chip_of(self, n):
        if isinstance(n, int):
            return self.chip_at((n + 1) // 2 * (2 * (n % 2) - 1))
        return self.chip_at(lax.div(n + 1, 2) * (2 * lax.rem(n, 2) - 1))

    def barrier(self):
        sem = pltpu.get_barrier_semaphore()
        peers = [self.next[0], self.next[1], self.sibling, self.ahead]
        if self.sections > 2:
            peers.append(self.behind)
        for who in peers:
            pl.semaphore_signal(sem, inc=1, device_id=who, device_id_type=pl.DeviceIdType.MESH)
        pl.semaphore_wait(sem, len(peers))


class Gather:
    def __init__(self, ring, whole, rows, sems):
        self.ring, self.whole, self.rows = ring, whole, rows
        self.send, self.recv, self.sib_send, self.sib_recv = sems
        self.each = ring.m // whole.shape[0]

    def at(self, chunk, first, size):
        start = (lax.rem(chunk, self.each) * 2 + self.ring.core) * self.rows + first
        return self.whole.at[lax.div(chunk, self.each), pl.ds(pl.multiple_of(start, size), size)]

    def part(self, chunk, u):
        return self.at(chunk, u * (self.rows // SUBS), self.rows // SUBS)

    def own(self):
        return self.at(self.ring.chip, 0, self.rows)

    def hop(self, d, s, u, ref):
        return remote(ref, ref, self.send.at[d, s, u], self.recv.at[d, s, u], self.ring.next[d])

    def over(self, d, s, u, ref):
        return remote(
            ref, ref, self.sib_send.at[d, s, u], self.sib_recv.at[d, s, u], self.ring.sibling
        )

    def start(self, u):
        half = self.ring.half
        refs = [self.part(self.ring.chip, v) for v in range(SUBS)]
        self.hop(u, 0, u, refs[u]).start()
        self.over(0, 0, u, refs[u]).start()
        if u and half > 1:
            for d in range(2):
                self.hop(d, 0, 1 - d, refs[1 - d]).start()

    def forward(self, s, v):
        half = self.ring.half
        for d in range(2):
            u = v if d == 0 else 1 - v
            ref = self.part(self.ring.chip_at(-s if d == 0 else s), u)

            def pass_on(d=d, u=u, ref=ref):
                self.hop(d, s - 1, u, ref).wait_recv()
                cond(
                    both(s < half, either(s < half - 1, v == 0)),
                    lambda: self.hop(d, s, u, ref).start(),
                )
                self.over(d, s, u, ref).start()

            cond(either(s < half, v == 0), pass_on)

    def ready(self, n):
        m, half = self.ring.m, self.ring.half
        ref = self.part(self.ring.chip, 0)

        def far():
            for d in range(2):
                self.over(d, half, d, ref).wait_recv()

        def near():
            d, s = lax.rem(n, 2), lax.div(n + 1, 2)
            for u in range(SUBS):
                self.over(d, s, u, ref).wait_recv()

        pl.when(n == m - 1)(far)
        pl.when(n != m - 1)(near)

    def run(self, work):
        m = self.ring.m

        def body(i):
            self.forward(lax.div(i, 2) + 1, lax.rem(i, 2))
            low = jnp.where(i > m - 3, i, jnp.maximum(i - 1, 0))
            many = jnp.where(i == 1, 0, jnp.where(i == m - 3, 2, 1))
            work(i, low, low + many)

        loop(0, m, body)

    def drain(self):
        half = self.ring.half
        ref = self.part(self.ring.chip, 0)
        for d in range(2):
            for u in range(SUBS):
                for s in range(half + 1):
                    if s < half and (s < half - 1 or u == d):
                        self.hop(d, s, u, ref).wait_send()
                    if (d == 0) if s == 0 else (s < half or u == d):
                        self.over(d, s, u, ref).wait_send()


class Scatter:
    def __init__(self, ring, own, give, land, buf, sems):
        self.ring, self.own, self.give, self.land, self.buf = ring, own, give, land, buf
        self.send, self.recv, self.sib_send, self.sib_recv = sems
        self.rows = own.shape[1] // SUBS

    def over(self, n, chunk):
        return remote(
            self.give.at[chunk], self.land.at[chunk], self.sib_send.at[n], self.sib_recv.at[n],
            self.ring.sibling,
        )

    def offer(self, n):
        self.over(n, self.ring.chip_of(n)).start()

    def settle(self, n):
        self.over(n, self.ring.chip).wait_recv()

    def move(self, d, j, u):
        return remote(
            self.buf.at[d, j, u], self.buf.at[d, j + 1, u], self.send.at[d, j, u],
            self.recv.at[d, j, u], self.ring.next[d],
        )

    def local(self, chunk, u):
        cut = pl.ds(pl.multiple_of(u * self.rows, self.rows), self.rows)
        return self.own[chunk, cut, :] + self.land[chunk, cut, :].astype(F32)

    def step(self, j, late):
        m, half = self.ring.m, self.ring.half
        dist = half - j
        if isinstance(j, int) and j == 0:
            self.settle(m - 1)
        elif not late:
            self.settle(2 * dist - 1)
            self.settle(2 * dist)
        fresh = isinstance(j, int) and j == (0 if late else 1)
        for d in range(2):
            u = d if late else 1 - d
            value = self.local(self.ring.chip_at(dist if d == 0 else -dist), u)
            if not fresh:
                self.move(d, j - 1, u).wait_recv()
                value = value + self.buf[d, j, u].astype(F32)
            self.buf[d, j, u] = value.astype(BF)
            self.move(d, j, u).start()

    def rest(self, slot, before=lambda q: None):
        half = self.ring.half

        def body(q):
            k = lax.div(q, 2)
            before(q)
            pl.when(jnp.logical_and(lax.rem(q, 2) == 0, k + 2 < half))(
                lambda: self.step(k + 2, False)
            )
            pl.when(lax.rem(q, 2) == 1)(lambda: self.step(k + 1, True))
            slot(q)

        loop(0, 2 * (half - 1), body)

    def last(self, u):
        half = self.ring.half
        if u == 0:
            self.settle(0)
        value = self.local(self.ring.chip, u)
        for d in range(2):
            if half > 1 or u == d:
                self.move(d, half - 1, u).wait_recv()
                value = value + self.buf[d, half, u].astype(F32)
        return value.astype(BF)

    def drain(self):
        for d in range(2):
            for u in range(SUBS):
                for j in range(self.ring.half):
                    if j or u == d:
                        self.move(d, j, u).wait_send()
        for n in range(self.ring.m):
            self.over(n, self.ring.chip).wait_send()


class Apply:
    def __init__(self, ring, rights, mixers, limits, pair, acc):
        self.ring, self.rights, self.acc = ring, rights, acc
        self.mixers, self.limits, self.pair = mixers, limits, pair
        self.terms, self.sectors, self.block, _ = rights.shape
        self.local = mixers.shape[2]

    def lift(self, t, q, left, v):
        return [
            jnp.dot(left, v[q, pl.ds(s * self.block, self.block), :], preferred_element_type=F32)
            .astype(BF)
            for s in range(self.local)
        ]

    def mix(self, t, q, x, lifted):
        live = jnp.where(q < self.limits[0, t], 1.0, 0.0).astype(F32)
        mixed = (live * self.mixers[0, t, x, 0]) * lifted[0].astype(F32)
        for y in range(1, self.local):
            mixed = mixed + (live * self.mixers[0, t, x, y]) * lifted[y].astype(F32)
        return mixed.astype(BF)

    def right(self, t, q, mixed):
        return lax.dot_general(
            mixed, self.rights[t, self.pair[0, q]], (((1,), (1,)), ((), ())),
            preferred_element_type=F32,
        )

    def to(self, q, v, left_of, st, given):
        per = self.local // 2
        lifted = [self.lift(t, q, left_of(t), v) for t in range(self.terms)]
        for i in range(self.local):
            core = 1 - self.ring.core if i < per else self.ring.core
            x = core * per + i % per
            total = None
            for t in range(self.terms):
                term = self.right(t, q, self.mix(t, q, x, lifted[t]))
                total = term if total is None else total + term
            rows = pl.ds(i % per * self.block, self.block)
            if i < per:
                st.give[q, rows, :] = total.astype(BF)
            else:
                st.own[q, rows, :] = total
            if i == per - 1:
                given()

    def shared(self, q, v, left_of, st):
        acc = self.acc
        for t in range(self.terms):
            lifted = self.lift(t, q, left_of(t), v)
            for x in range(self.local):
                rows = pl.ds(x * self.block, self.block)
                term = self.right(t, q, self.mix(t, q, x, lifted))
                acc[rows, :] = term if t == 0 else acc[rows, :] + term
        rows = st.own.shape[1]
        each = st.own.shape[0] // self.sectors
        core = self.ring.core
        for j in range(each):
            mine = pl.multiple_of((2 * j + core) * rows, rows)
            other = pl.multiple_of((2 * j + 1 - core) * rows, rows)
            st.own[q * each + j] = acc[pl.ds(mine, rows), :]
            st.give[q * each + j] = acc[pl.ds(other, rows), :].astype(BF)


def renew(i, j, pair, lefts, tensor, out):
    terms, sectors = lefts.shape[:2]
    local = tensor.shape[1]
    source = jnp.int32(0)
    for k in range(sectors):
        source = jnp.where(pair[0, k] == j, k, source)
    stack = jnp.concatenate([tensor[source, s] for s in range(local)], axis=0)
    for t in range(terms):
        lifted = [
            jnp.dot(lefts[t, source], tensor[source, s], preferred_element_type=F32).astype(BF)
            for s in range(local)
        ]
        out[i, t] = lax.dot_general(
            stack, jnp.concatenate(lifted, axis=0), (((0,), (0,)), ((), ())),
            preferred_element_type=F32,
        ).astype(BF)


def interleaved(chips, sectors, local):
    return chips == sectors and chips == 8 and local % 2 == 0


def whole_kernel(
    count, sections, pair, limits, mixers, wave, left_in, right_in, tensor_in,
    out1, out2, out3,
    lefts, rights, tensor, whole, image, renewed, moved, acc, stage,
    loads, writes, cross_send, cross_recv, *rest
):
    ring = Ring(count, sections)
    m, half, core = ring.m, ring.half, ring.core
    terms, sectors = rights.shape[:2]
    rows = wave.shape[0]
    tight = interleaved(m, sectors, mixers.shape[2])
    s1, s2, s3 = (
        Scatter(ring, *rest[8 * i:8 * i + 4], rest[8 * i + 4:8 * i + 8]) for i in range(3)
    )
    g1 = Gather(ring, whole, rows, rest[24:28])
    g2 = Gather(ring, image, rows, rest[28:32])
    work = Apply(ring, rights, mixers, limits, pair, acc)

    keep = pltpu.make_async_copy(wave, g1.own(), loads.at[3])
    keep.start()
    loaded = [
        pltpu.make_async_copy(a, b, loads.at[i])
        for i, (a, b) in enumerate(((left_in, lefts), (tensor_in, tensor), (right_in, rights)))
    ]
    for copy in loaded:
        copy.start()
    ring.barrier()
    keep.wait()
    for u in range(SUBS):
        g1.start(u)
    def sector_of(i):
        return ring.chip_of(m - 1 - i) if tight else i

    def crossing(i):
        return remote(
            renewed.at[i], moved.at[i], cross_send.at[i], cross_recv.at[i], ring.ahead
        )

    def renew_one(i):
        renew(i, sector_of(i), pair, lefts, tensor, renewed)
        crossing(i).start()

    def apply_to(st, v, n):
        work.to(ring.chip_of(n), v, lambda t: lefts[t, ring.chip_of(n)], st, lambda: st.offer(n))

    def apply_moved(i):
        crossing(i).wait_recv()
        n = m - 1 - i
        work.to(ring.chip_of(n), whole, lambda t: moved[i, t], s3, lambda: s3.offer(n))

    def finish(st, ref, after=lambda u: None):
        size = rows // SUBS
        for u in range(SUBS):
            ref[pl.ds(u * size, size), :] = st.last(u)
            after(u)

    def write(i, src, dst):
        pltpu.make_async_copy(src, dst, writes.at[i]).start()

    for copy in loaded:
        copy.wait()
    if tight:
        def sectors_in(g, st, v, low, high):
            def body(n):
                g.ready(n)
                apply_to(st, v, n)

            lax.fori_loop(low, high, lambda n, c: body(n) or c, 0)

        def first_work(i, low, high):
            pl.when(jnp.logical_or(i == 0, jnp.logical_and(lax.rem(i, 2) == 1, i < m - 3)))(
                lambda: renew_one(lax.div(i + 1, 2))
            )
            pl.when(i == m - 1)(lambda: s1.step(1, False))
            sectors_in(g1, s1, whole, low, high)

        g1.run(first_work)
        s1.step(0, True)

        def first_slot(q):
            pl.when(q < half + 1)(lambda: renew_one(half - 1 + q))
            pl.when(jnp.logical_or(q == 0, jnp.logical_or(q == 3, q == 4)))(
                lambda: apply_moved(jnp.maximum(q - 2, 0))
            )

        s1.rest(first_slot, lambda q: pl.when(q == 5)(lambda: s3.step(0, True)))
        s3.step(1, False)
        finish(s1, g2.own(), g2.start)
        write(0, g2.own(), out1)

        def second_work(i, low, high):
            def turn():
                s3.step(1, True)
                s3.step(2, False)

            pl.when(i == m - 4)(turn)
            pl.when(i == m - 1)(lambda: s2.step(1, False))
            sectors_in(g2, s2, image, low, high)
            pl.when(jnp.logical_or(i == 1, i == 3))(lambda: apply_moved(3 + lax.div(i, 2)))

        g2.run(second_work)
        s2.step(0, True)
        s3.step(2, True)

        def second_slot(q):
            pl.when(q == 2)(lambda: s3.step(3, False))
            pl.when(q < 3)(lambda: apply_moved(5 + q))

        s2.rest(second_slot, lambda q: pl.when(q == 5)(lambda: s3.step(3, True)))
        finish(s3, stage.at[1])
        write(2, stage.at[1], out3)
        finish(s2, stage.at[0])
        write(1, stage.at[0], out2)
    else:
        def plain(g):
            g.run(lambda i, low, high: None)
            loop(0, m, g.ready)

        def spread(st, v, left_of, before=lambda q: None):
            def body(q):
                before(q)
                work.shared(q, v, functools.partial(left_of, q), st)

            loop(0, sectors, body)
            loop(0, m, st.offer)
            st.step(0, True)
            if half > 1:
                st.step(1, False)
            st.rest(lambda q: None)

        def plain_left(q, t):
            return lefts[t, q]

        loop(0, sectors, renew_one)
        plain(g1)
        spread(s1, whole, plain_left)
        finish(s1, g2.own(), g2.start)
        write(0, g2.own(), out1)
        plain(g2)
        spread(s2, image, plain_left)
        finish(s2, stage.at[0])
        write(1, stage.at[0], out2)
        spread(s3, whole, lambda q, t: moved[q, t], lambda q: crossing(q).wait_recv())
        finish(s3, stage.at[1])
        write(2, stage.at[1], out3)
    for part in (g1, g2, s1, s2, s3):
        part.drain()
    loop(0, sectors, lambda i: crossing(i).wait_send())
    for i, out in enumerate((out1, out2, out3)):
        pltpu.make_async_copy(stage.at[0], out, writes.at[i]).wait()


def hand_out(*refs):
    ins, outs, (held, loads, writes) = refs[:3], refs[3:6], refs[6:]
    copies = [pltpu.make_async_copy(a, held.at[i], loads.at[i]) for i, a in enumerate(ins)]
    for copy in copies:
        copy.start()
    back = []
    for i, copy in enumerate(copies):
        copy.wait()
        back.append(pltpu.make_async_copy(held.at[i], outs[i], writes.at[i]))
        back[-1].start()
    for copy in back:
        copy.wait()


def gather_scratch(half):
    dma = pltpu.SemaphoreType.DMA
    hop, sib = (2, half, SUBS), (2, half + 1, SUBS)
    return [dma(hop), dma(hop), dma(sib), dma(sib)]


def scatter_scratch(chips, rows, width):
    half = chips // 2
    dma = pltpu.SemaphoreType.DMA
    hop = (2, half, SUBS)
    return [
        pltpu.VMEM((chips, rows, width), F32),
        pltpu.VMEM((chips, rows, width), BF),
        pltpu.VMEM((chips, rows, width), BF),
        pltpu.VMEM((2, half + 1, SUBS, rows // SUBS, width), BF),
        dma(hop), dma(hop), dma((chips,)), dma((chips,)),
    ]


def shards(count, sections, wave, left_ops, right_ops, site_ops, reach, pairing, site_tensor):
    lefts, rights, own, tensor = left_ops[0], right_ops[0], wave[0], site_tensor[0]
    terms, sectors, block, _ = lefts.shape
    rows, width = own.shape
    chips = count // 2
    height = count * rows // sectors
    tight = interleaved(chips, sectors, site_ops.shape[2])
    dma = pltpu.SemaphoreType.DMA
    sm = pl.BlockSpec(memory_space=pltpu.SMEM)
    anyw = pl.BlockSpec(memory_space=pl.ANY)
    image = pltpu.VMEM((sectors, height, width), BF)
    across = pltpu.VMEM((sectors, terms, block, block), BF)
    mine = jax.ShapeDtypeStruct((rows, width), BF)
    outs = pl.pallas_call(
        functools.partial(whole_kernel, count, sections),
        out_shape=[mine] * 3,
        in_specs=[sm] * 3 + [anyw] * 4,
        out_specs=[anyw] * 3,
        scratch_shapes=[
            pltpu.VMEM(lefts.shape, BF), pltpu.VMEM(rights.shape, BF),
            pltpu.VMEM(tensor.shape, BF), image, image, across, across,
            pltpu.VMEM((8, width) if tight else (height, width), F32),
            pltpu.VMEM((2, rows, width), BF),
            dma((4,)), dma((3,)), dma((sectors,)), dma((sectors,)),
        ] + scatter_scratch(chips, rows, width) * 3 + gather_scratch(chips // 2) * 2,
        compiler_params=pltpu.CompilerParams(
            collective_id=0, has_side_effects=True, vmem_limit_bytes=BIG
        ),
        name="images",
    )(pairing, reach, site_ops, own, lefts, rights, tensor)
    outs = pl.pallas_call(
        hand_out,
        out_shape=[mine] * 3,
        in_specs=[anyw] * 3,
        out_specs=[anyw] * 3,
        scratch_shapes=[pltpu.VMEM((3, rows, width), BF), dma((3,)), dma((3,))],
        name="hand_out",
    )(*outs)
    return tuple(out[None] for out in outs)


def solution(mesh):
    placed = (
        P("sect", "op", None),
        P("sect", "op", None, None, None),
        P("sect", "op", None, None, None),
        P("sect", "op", None, None),
        P("sect", "op"),
        P("sect", None),
        P("sect", None, None, None, None),
    )
    return jax.shard_map(
        functools.partial(shards, mesh.shape["op"], mesh.shape["sect"]),
        mesh=mesh,
        in_specs=placed,
        out_specs=(P("sect", "op", None), P("sect", "op", None), P("sect", "op", None)),
        check_vma=False,
    )
```

```python
import functools

import jax
import jax.numpy as jnp
from jax import lax
from jax.experimental import pallas as pl
from jax.experimental.pallas import tpu as pltpu
from jax.sharding import PartitionSpec as P

SUBS = 2
BIG = 67043328
BF, F32 = jnp.bfloat16, jnp.float32


def remote(src, dst, send, recv, who):
    return pltpu.make_async_remote_copy(
        src_ref=src, dst_ref=dst, send_sem=send, recv_sem=recv, device_id=who,
        device_id_type=pl.DeviceIdType.MESH,
    )


def cond(test, body):
    if isinstance(test, bool):
        if test:
            body()
    else:
        pl.when(test)(body)


def both(a, b):
    return (a and b) if isinstance(a, bool) and isinstance(b, bool) else jnp.logical_and(a, b)


def either(a, b):
    return (a or b) if isinstance(a, bool) and isinstance(b, bool) else jnp.logical_or(a, b)


def loop(low, high, body):
    if low < high:
        lax.fori_loop(low, high, lambda i, c: body(i) or c, 0)


class Ring:
    def __init__(self, count, sections):
        me = lax.axis_index("op")
        here = lax.axis_index("sect")
        self.sections = sections
        self.ahead = {"sect": lax.rem(here + 1, sections)}
        self.behind = {"sect": lax.rem(here + sections - 1, sections)}
        self.m = count // 2
        self.half = self.m // 2
        self.core = lax.rem(me, 2)
        self.chip = lax.div(me, 2)
        odd = lax.rem(self.chip, 2)
        low = lax.div(self.chip, 2)
        self.pos = (1 - odd) * low + odd * (self.m - 1 - low)
        self.sibling = {"op": self.chip * 2 + 1 - self.core}
        self.next = [
            {"op": self.chip_at(1) * 2 + self.core},
            {"op": self.chip_at(-1) * 2 + self.core},
        ]

    def chip_at(self, offset):
        pos = lax.rem(self.pos + offset + self.m, self.m)
        upper = lax.div(pos, self.half)
        return (1 - upper) * (2 * pos) + upper * (2 * (self.m - 1 - pos) + 1)

    def chip_of(self, n):
        if isinstance(n, int):
            return self.chip_at((n + 1) // 2 * (2 * (n % 2) - 1))
        return self.chip_at(lax.div(n + 1, 2) * (2 * lax.rem(n, 2) - 1))

    def barrier(self):
        sem = pltpu.get_barrier_semaphore()
        peers = [self.next[0], self.next[1], self.sibling, self.ahead]
        if self.sections > 2:
            peers.append(self.behind)
        for who in peers:
            pl.semaphore_signal(sem, inc=1, device_id=who, device_id_type=pl.DeviceIdType.MESH)
        pl.semaphore_wait(sem, len(peers))


class Gather:
    def __init__(self, ring, whole, rows, sems):
        self.ring, self.whole, self.rows = ring, whole, rows
        self.send, self.recv, self.sib_send, self.sib_recv = sems
        self.each = ring.m // whole.shape[0]

    def at(self, chunk, first, size):
        start = (lax.rem(chunk, self.each) * 2 + self.ring.core) * self.rows + first
        return self.whole.at[lax.div(chunk, self.each), pl.ds(pl.multiple_of(start, size), size)]

    def part(self, chunk, u):
        return self.at(chunk, u * (self.rows // SUBS), self.rows // SUBS)

    def own(self):
        return self.at(self.ring.chip, 0, self.rows)

    def hop(self, d, s, u, ref):
        return remote(ref, ref, self.send.at[d, s, u], self.recv.at[d, s, u], self.ring.next[d])

    def over(self, d, s, u, ref):
        return remote(
            ref, ref, self.sib_send.at[d, s, u], self.sib_recv.at[d, s, u], self.ring.sibling
        )

    def start(self, u):
        half = self.ring.half
        refs = [self.part(self.ring.chip, v) for v in range(SUBS)]
        self.hop(u, 0, u, refs[u]).start()
        self.over(0, 0, u, refs[u]).start()
        if u and half > 1:
            for d in range(2):
                self.hop(d, 0, 1 - d, refs[1 - d]).start()

    def forward(self, s, v):
        half = self.ring.half
        for d in range(2):
            u = v if d == 0 else 1 - v
            ref = self.part(self.ring.chip_at(-s if d == 0 else s), u)

            def pass_on(d=d, u=u, ref=ref):
                self.hop(d, s - 1, u, ref).wait_recv()
                cond(
                    both(s < half, either(s < half - 1, v == 0)),
                    lambda: self.hop(d, s, u, ref).start(),
                )
                self.over(d, s, u, ref).start()

            cond(either(s < half, v == 0), pass_on)

    def ready(self, n):
        m, half = self.ring.m, self.ring.half
        ref = self.part(self.ring.chip, 0)

        def far():
            for d in range(2):
                self.over(d, half, d, ref).wait_recv()

        def near():
            d, s = lax.rem(n, 2), lax.div(n + 1, 2)
            for u in range(SUBS):
                self.over(d, s, u, ref).wait_recv()

        pl.when(n == m - 1)(far)
        pl.when(n != m - 1)(near)

    def run(self, work):
        m = self.ring.m

        def body(i):
            self.forward(lax.div(i, 2) + 1, lax.rem(i, 2))
            low = jnp.where(i > m - 3, i, jnp.maximum(i - 1, 0))
            many = jnp.where(i == 1, 0, jnp.where(i == m - 3, 2, 1))
            work(i, low, low + many)

        loop(0, m, body)

    def drain(self):
        half = self.ring.half
        ref = self.part(self.ring.chip, 0)
        for d in range(2):
            for u in range(SUBS):
                for s in range(half + 1):
                    if s < half and (s < half - 1 or u == d):
                        self.hop(d, s, u, ref).wait_send()
                    if (d == 0) if s == 0 else (s < half or u == d):
                        self.over(d, s, u, ref).wait_send()


class Scatter:
    def __init__(self, ring, own, give, land, buf, sems):
        self.ring, self.own, self.give, self.land, self.buf = ring, own, give, land, buf
        self.send, self.recv, self.sib_send, self.sib_recv = sems
        self.rows = own.shape[1] // SUBS

    def over(self, n, chunk):
        return remote(
            self.give.at[chunk], self.land.at[chunk], self.sib_send.at[n], self.sib_recv.at[n],
            self.ring.sibling,
        )

    def offer(self, n):
        self.over(n, self.ring.chip_of(n)).start()

    def settle(self, n):
        self.over(n, self.ring.chip).wait_recv()

    def move(self, d, j, u):
        return remote(
            self.buf.at[d, j, u], self.buf.at[d, j + 1, u], self.send.at[d, j, u],
            self.recv.at[d, j, u], self.ring.next[d],
        )

    def local(self, chunk, u):
        cut = pl.ds(pl.multiple_of(u * self.rows, self.rows), self.rows)
        return self.own[chunk, cut, :] + self.land[chunk, cut, :].astype(F32)

    def step(self, j, late):
        m, half = self.ring.m, self.ring.half
        dist = half - j
        if isinstance(j, int) and j == 0:
            self.settle(m - 1)
        elif not late:
            self.settle(2 * dist - 1)
            self.settle(2 * dist)
        fresh = isinstance(j, int) and j == (0 if late else 1)
        for d in range(2):
            u = d if late else 1 - d
            value = self.local(self.ring.chip_at(dist if d == 0 else -dist), u)
            if not fresh:
                self.move(d, j - 1, u).wait_recv()
                value = value + self.buf[d, j, u].astype(F32)
            self.buf[d, j, u] = value.astype(BF)
            self.move(d, j, u).start()

    def rest(self, slot, before=lambda q: None):
        half = self.ring.half

        def body(q):
            k = lax.div(q, 2)
            before(q)
            pl.when(jnp.logical_and(lax.rem(q, 2) == 0, k + 2 < half))(
                lambda: self.step(k + 2, False)
            )
            pl.when(lax.rem(q, 2) == 1)(lambda: self.step(k + 1, True))
            slot(q)

        loop(0, 2 * (half - 1), body)

    def last(self, u):
        half = self.ring.half
        if u == 0:
            self.settle(0)
        value = self.local(self.ring.chip, u)
        for d in range(2):
            if half > 1 or u == d:
                self.move(d, half - 1, u).wait_recv()
                value = value + self.buf[d, half, u].astype(F32)
        return value.astype(BF)

    def drain(self):
        for d in range(2):
            for u in range(SUBS):
                for j in range(self.ring.half):
                    if j or u == d:
                        self.move(d, j, u).wait_send()
        for n in range(self.ring.m):
            self.over(n, self.ring.chip).wait_send()


class Apply:
    def __init__(self, ring, rights, mixers, limits, pair, acc):
        self.ring, self.rights, self.acc = ring, rights, acc
        self.mixers, self.limits, self.pair = mixers, limits, pair
        self.terms, self.sectors, self.block, _ = rights.shape
        self.local = mixers.shape[2]

    def lift(self, t, q, left, v):
        return [
            jnp.dot(left, v[q, pl.ds(s * self.block, self.block), :], preferred_element_type=F32)
            .astype(BF)
            for s in range(self.local)
        ]

    def mix(self, t, q, x, lifted):
        live = jnp.where(q < self.limits[0, t], 1.0, 0.0).astype(F32)
        mixed = (live * self.mixers[0, t, x, 0]) * lifted[0].astype(F32)
        for y in range(1, self.local):
            mixed = mixed + (live * self.mixers[0, t, x, y]) * lifted[y].astype(F32)
        return mixed.astype(BF)

    def right(self, t, q, mixed):
        return lax.dot_general(
            mixed, self.rights[t, self.pair[0, q]], (((1,), (1,)), ((), ())),
            preferred_element_type=F32,
        )

    def to(self, q, v, left_of, st, given):
        per = self.local // 2
        lifted = [self.lift(t, q, left_of(t), v) for t in range(self.terms)]
        for i in range(self.local):
            core = 1 - self.ring.core if i < per else self.ring.core
            x = core * per + i % per
            total = None
            for t in range(self.terms):
                term = self.right(t, q, self.mix(t, q, x, lifted[t]))
                total = term if total is None else total + term
            rows = pl.ds(i % per * self.block, self.block)
            if i < per:
                st.give[q, rows, :] = total.astype(BF)
            else:
                st.own[q, rows, :] = total
            if i == per - 1:
                given()

    def shared(self, q, v, left_of, st):
        acc = self.acc
        for t in range(self.terms):
            lifted = self.lift(t, q, left_of(t), v)
            for x in range(self.local):
                rows = pl.ds(x * self.block, self.block)
                term = self.right(t, q, self.mix(t, q, x, lifted))
                acc[rows, :] = term if t == 0 else acc[rows, :] + term
        rows = st.own.shape[1]
        each = st.own.shape[0] // self.sectors
        core = self.ring.core
        for j in range(each):
            mine = pl.multiple_of((2 * j + core) * rows, rows)
            other = pl.multiple_of((2 * j + 1 - core) * rows, rows)
            st.own[q * each + j] = acc[pl.ds(mine, rows), :]
            st.give[q * each + j] = acc[pl.ds(other, rows), :].astype(BF)


def renew(i, j, pair, lefts, tensor, out):
    terms, sectors = lefts.shape[:2]
    local = tensor.shape[1]
    source = jnp.int32(0)
    for k in range(sectors):
        source = jnp.where(pair[0, k] == j, k, source)
    stack = jnp.concatenate([tensor[source, s] for s in range(local)], axis=0)
    for t in range(terms):
        lifted = [
            jnp.dot(lefts[t, source], tensor[source, s], preferred_element_type=F32).astype(BF)
            for s in range(local)
        ]
        out[i, t] = lax.dot_general(
            stack, jnp.concatenate(lifted, axis=0), (((0,), (0,)), ((), ())),
            preferred_element_type=F32,
        ).astype(BF)


def interleaved(chips, sectors, local):
    return chips == sectors and chips == 8 and local % 2 == 0


def whole_kernel(
    count, sections, pair_in, limits_in, mixers_in, wave, left_in, right_in, tensor_in,
    out1, out2, out3,
    pair, limits, mixers, lefts, rights, tensor, whole, image, renewed, moved, acc, stage,
    loads, writes, cross_send, cross_recv, *rest
):
    ring = Ring(count, sections)
    m, half, core = ring.m, ring.half, ring.core
    terms, sectors = rights.shape[:2]
    rows = wave.shape[0]
    tight = interleaved(m, sectors, mixers.shape[2])
    s1, s2, s3 = (
        Scatter(ring, *rest[8 * i:8 * i + 4], rest[8 * i + 4:8 * i + 8]) for i in range(3)
    )
    g1 = Gather(ring, whole, rows, rest[24:28])
    g2 = Gather(ring, image, rows, rest[28:32])
    work = Apply(ring, rights, mixers, limits, pair, acc)

    keep = pltpu.make_async_copy(wave, g1.own(), loads.at[3])
    keep.start()
    scalars = [
        pltpu.make_async_copy(a, b, loads.at[i])
        for i, (a, b) in enumerate(((pair_in, pair), (limits_in, limits), (mixers_in, mixers)), 4)
    ]
    for copy in scalars:
        copy.start()
    loaded = [
        pltpu.make_async_copy(a, b, loads.at[i])
        for i, (a, b) in enumerate(((left_in, lefts), (tensor_in, tensor), (right_in, rights)))
    ]
    for copy in loaded:
        copy.start()
    ring.barrier()
    keep.wait()
    for u in range(SUBS):
        g1.start(u)
    def sector_of(i):
        return ring.chip_of(m - 1 - i) if tight else i

    def crossing(i):
        return remote(
            renewed.at[i], moved.at[i], cross_send.at[i], cross_recv.at[i], ring.ahead
        )

    def renew_one(i):
        renew(i, sector_of(i), pair, lefts, tensor, renewed)
        crossing(i).start()

    def apply_to(st, v, n):
        work.to(ring.chip_of(n), v, lambda t: lefts[t, ring.chip_of(n)], st, lambda: st.offer(n))

    def apply_moved(i):
        crossing(i).wait_recv()
        n = m - 1 - i
        work.to(ring.chip_of(n), whole, lambda t: moved[i, t], s3, lambda: s3.offer(n))

    def finish(st, ref, after=lambda u: None):
        size = rows // SUBS
        for u in range(SUBS):
            ref[pl.ds(u * size, size), :] = st.last(u)
            after(u)

    def write(i, src, dst):
        pltpu.make_async_copy(src, dst, writes.at[i]).start()

    for copy in scalars + loaded:
        copy.wait()
    if tight:
        def sectors_in(g, st, v, low, high):
            def body(n):
                g.ready(n)
                apply_to(st, v, n)

            lax.fori_loop(low, high, lambda n, c: body(n) or c, 0)

        def first_work(i, low, high):
            pl.when(jnp.logical_or(i == 0, jnp.logical_and(lax.rem(i, 2) == 1, i < m - 3)))(
                lambda: renew_one(lax.div(i + 1, 2))
            )
            pl.when(i == m - 1)(lambda: s1.step(1, False))
            sectors_in(g1, s1, whole, low, high)

        g1.run(first_work)
        s1.step(0, True)
        loop(0, 2, apply_moved)

        def first_slot(q):
            pl.when(q < half + 1)(lambda: renew_one(half - 1 + q))
            pl.when(q == half + 1)(lambda: apply_moved(2))

        s1.rest(first_slot, lambda q: pl.when(q == 5)(lambda: s3.step(0, True)))
        s3.step(1, False)
        finish(s1, g2.own(), g2.start)
        write(0, g2.own(), out1)

        def second_work(i, low, high):
            def turn():
                s3.step(1, True)
                s3.step(2, False)

            pl.when(i == m - 4)(turn)
            pl.when(i == m - 1)(lambda: s2.step(1, False))
            sectors_in(g2, s2, image, low, high)
            pl.when(jnp.logical_or(i == 1, i == 3))(lambda: apply_moved(3 + lax.div(i, 2)))

        g2.run(second_work)
        s2.step(0, True)
        s3.step(2, True)

        def second_slot(q):
            pl.when(q == 2)(lambda: s3.step(3, False))
            pl.when(q < 3)(lambda: apply_moved(5 + q))

        s2.rest(second_slot, lambda q: pl.when(q == 5)(lambda: s3.step(3, True)))
        finish(s3, stage.at[1])
        write(2, stage.at[1], out3)
        finish(s2, stage.at[0])
        write(1, stage.at[0], out2)
    else:
        def plain(g):
            g.run(lambda i, low, high: None)
            loop(0, m, g.ready)

        def spread(st, v, left_of, before=lambda q: None):
            def body(q):
                before(q)
                work.shared(q, v, functools.partial(left_of, q), st)

            loop(0, sectors, body)
            loop(0, m, st.offer)
            st.step(0, True)
            if half > 1:
                st.step(1, False)
            st.rest(lambda q: None)

        def plain_left(q, t):
            return lefts[t, q]

        loop(0, sectors, renew_one)
        plain(g1)
        spread(s1, whole, plain_left)
        finish(s1, g2.own(), g2.start)
        write(0, g2.own(), out1)
        plain(g2)
        spread(s2, image, plain_left)
        finish(s2, stage.at[0])
        write(1, stage.at[0], out2)
        spread(s3, whole, lambda q, t: moved[q, t], lambda q: crossing(q).wait_recv())
        finish(s3, stage.at[1])
        write(2, stage.at[1], out3)
    for part in (g1, g2, s1, s2, s3):
        part.drain()
    loop(0, sectors, lambda i: crossing(i).wait_send())
    for i, out in enumerate((out1, out2, out3)):
        pltpu.make_async_copy(stage.at[0], out, writes.at[i]).wait()


def hand_out(*refs):
    ins, outs, (held, loads, writes) = refs[:3], refs[3:6], refs[6:]
    copies = [pltpu.make_async_copy(a, held.at[i], loads.at[i]) for i, a in enumerate(ins)]
    for copy in copies:
        copy.start()
    back = []
    for i, copy in enumerate(copies):
        copy.wait()
        back.append(pltpu.make_async_copy(held.at[i], outs[i], writes.at[i]))
        back[-1].start()
    for copy in back:
        copy.wait()


def gather_scratch(half):
    dma = pltpu.SemaphoreType.DMA
    hop, sib = (2, half, SUBS), (2, half + 1, SUBS)
    return [dma(hop), dma(hop), dma(sib), dma(sib)]


def scatter_scratch(chips, rows, width):
    half = chips // 2
    dma = pltpu.SemaphoreType.DMA
    hop = (2, half, SUBS)
    return [
        pltpu.VMEM((chips, rows, width), F32),
        pltpu.VMEM((chips, rows, width), BF),
        pltpu.VMEM((chips, rows, width), BF),
        pltpu.VMEM((2, half + 1, SUBS, rows // SUBS, width), BF),
        dma(hop), dma(hop), dma((chips,)), dma((chips,)),
    ]


def shards(count, sections, wave, left_ops, right_ops, site_ops, reach, pairing, site_tensor):
    lefts, rights, own, tensor = left_ops[0], right_ops[0], wave[0], site_tensor[0]
    terms, sectors, block, _ = lefts.shape
    rows, width = own.shape
    chips = count // 2
    height = count * rows // sectors
    tight = interleaved(chips, sectors, site_ops.shape[2])
    dma = pltpu.SemaphoreType.DMA
    anyw = pl.BlockSpec(memory_space=pl.ANY)
    image = pltpu.VMEM((sectors, height, width), BF)
    across = pltpu.VMEM((sectors, terms, block, block), BF)
    mine = jax.ShapeDtypeStruct((rows, width), BF)
    outs = pl.pallas_call(
        functools.partial(whole_kernel, count, sections),
        out_shape=[mine] * 3,
        in_specs=[anyw] * 7,
        out_specs=[anyw] * 3,
        scratch_shapes=[
            pltpu.SMEM(pairing.shape, jnp.int32), pltpu.SMEM(reach.shape, jnp.int32),
            pltpu.SMEM(site_ops.shape, F32), pltpu.VMEM(lefts.shape, BF), pltpu.VMEM(rights.shape, BF),
            pltpu.VMEM(tensor.shape, BF), image, image, across, across,
            pltpu.VMEM((8, width) if tight else (height, width), F32),
            pltpu.VMEM((2, rows, width), BF),
            dma((7,)), dma((3,)), dma((sectors,)), dma((sectors,)),
        ] + scatter_scratch(chips, rows, width) * 3 + gather_scratch(chips // 2) * 2,
        compiler_params=pltpu.CompilerParams(
            collective_id=0, has_side_effects=True, vmem_limit_bytes=BIG
        ),
        name="images",
    )(pairing, reach, site_ops, own, lefts, rights, tensor)
    outs = pl.pallas_call(
        hand_out,
        out_shape=[mine] * 3,
        in_specs=[anyw] * 3,
        out_specs=[anyw] * 3,
        scratch_shapes=[pltpu.VMEM((3, rows, width), BF), dma((3,)), dma((3,))],
        name="hand_out",
    )(*outs)
    return tuple(out[None] for out in outs)


def solution(mesh):
    placed = (
        P("sect", "op", None),
        P("sect", "op", None, None, None),
        P("sect", "op", None, None, None),
        P("sect", "op", None, None),
        P("sect", "op"),
        P("sect", None),
        P("sect", None, None, None, None),
    )
    return jax.shard_map(
        functools.partial(shards, mesh.shape["op"], mesh.shape["sect"]),
        mesh=mesh,
        in_specs=placed,
        out_specs=(P("sect", "op", None), P("sect", "op", None), P("sect", "op", None)),
        check_vma=False,
    )
```
